32 devices in a mesh: expert: 4 (over y, x), cuts: 8 (over z, core).
Axes of the slice: x: 2, y: 2, z: 4, core: 2. Of those that a mesh axis runs over, the one named last changes fastest.
Arguments:
- token_rows: bfloat16 [4, 1152, 4096], P('expert', 'cuts'), may hold values from -6 to 6
- cotangent: bfloat16 [4, 1152, 4096], P('expert', 'cuts'), may hold values from -6 to 6
- counts: int32 [4], replicated, may hold values from 384 to 1152, as said below
- gate_master: float32 [4, 1152, 4096], P(None, 'cuts', 'expert'), may hold values from -0.09375 to 0.09375
- up_master: float32 [4, 1152, 4096], P(None, 'cuts', 'expert'), may hold values from -0.09375 to 0.09375
- down_master: float32 [4, 1152, 4096], P(None, 'cuts', 'expert'), may hold values from -0.1875 to 0.1875
- gate_first: float32 [4, 1152, 4096], P(None, 'cuts', 'expert'), may hold values from -60 to 60
- up_first: float32 [4, 1152, 4096], P(None, 'cuts', 'expert'), may hold values from -60 to 60
- down_first: float32 [4, 1152, 4096], P(None, 'cuts', 'expert'), may hold values from -60 to 60
- gate_second: float32 [4, 1152, 4096], P(None, 'cuts', 'expert'), may hold values from 100 to 1000
- up_second: float32 [4, 1152, 4096], P(None, 'cuts', 'expert'), may hold values from 100 to 1000
- down_second: float32 [4, 1152, 4096], P(None, 'cuts', 'expert'), may hold values from 100 to 1000
Outputs:
- out_rows: bfloat16 [4, 1152, 4096], P('expert', 'cuts')
- input_grads: bfloat16 [4, 1152, 4096], P('expert', 'cuts')
- new_gate_master: float32 [4, 1152, 4096], P(None, 'cuts', 'expert')
- new_up_master: float32 [4, 1152, 4096], P(None, 'cuts', 'expert')
- new_down_master: float32 [4, 1152, 4096], P(None, 'cuts', 'expert')
- new_gate_first: float32 [4, 1152, 4096], P(None, 'cuts', 'expert')
- new_up_first: float32 [4, 1152, 4096], P(None, 'cuts', 'expert')
- new_down_first: float32 [4, 1152, 4096], P(None, 'cuts', 'expert')
- new_gate_second: float32 [4, 1152, 4096], P(None, 'cuts', 'expert')
- new_up_second: float32 [4, 1152, 4096], P(None, 'cuts', 'expert')
- new_down_second: float32 [4, 1152, 4096], P(None, 'cuts', 'expert')
The draws below stay inside these ranges and needn't reach their ends.
Inputs may be any that keep to these rules, and one draw needn't show every extreme that they name: `counts`: some expert has exactly 1152 live rows in every draw.
All inputs are finite; a program needn't handle non-finite values.
Results may differ from the reference program's by a relative error of at most 0.015.
Values may be sent and summed in bfloat16 or wider, within the bound.
No kernel may reach another device: no remote copies, remote signals or barrier semaphores. Data moves between devices by JAX's collectives and lax.ppermute only.
A program may use at most 192 MiB of HBM per device.

```python
import math
import jax
import jax.numpy as jnp
from jax import lax

D = 4096
H = 1152
CAP = 1152
EXPERTS = 4
N_CUTS = 8


def draw_counts(key, part):
    first_key = jax.random.fold_in(key, 11)
    second_key = jax.random.fold_in(key, 23)
    values = jax.random.randint(first_key, (EXPERTS,), (CAP + 2) // 3, CAP + 1, dtype=jnp.int32)
    chosen = jax.random.randint(second_key, (), 0, EXPERTS, dtype=jnp.int32)
    position = jnp.arange(EXPERTS, dtype=jnp.int32)
    return jnp.where(position == chosen, jnp.int32(CAP), values).astype(jnp.int32)


def block_scale(own_key, shape, split, low, top_value):
    loudness, own = 1.0, jax.random.fold_in(own_key, 6)
    for dim, blocks in split:
        draws = jnp.exp(jax.random.uniform(jax.random.fold_in(own, dim), (blocks,), jnp.float32, low / len(split), top_value / len(split)))
        loudness = loudness * jnp.repeat(draws, shape[dim] // blocks).reshape([-1 if axis == dim else 1 for axis in range(len(shape))])
    return loudness


def noise(key, extent, scale, reach, shards=(), held_as=jnp.bfloat16):
    drawn = scale * jax.random.normal(key, extent, jnp.float32)
    if shards:
        drawn = drawn * block_scale(key, extent, shards, -0.22, 0.18)
    return jnp.clip(drawn, -reach, reach).astype(held_as)


def setup_inputs(seed: int = 0) -> dict:
    keys = jax.random.split(jax.random.key(seed), 13)
    return {
        "token_rows": noise(keys[0], (EXPERTS, CAP, D), 1.0, 6.0, ((0, 4), (1, 8))),
        "cotangent": noise(keys[1], (EXPERTS, CAP, D), 1.0, 6.0, ((0, 4), (1, 8))),
        "counts": draw_counts(jax.random.fold_in(keys[12], 71), 0),
        "gate_master": noise(keys[3], (EXPERTS, H, D), D ** -0.5, 0.09375, ((1, 8), (2, 4)), jnp.float32),
        "up_master": noise(keys[4], (EXPERTS, H, D), D ** -0.5, 0.09375, ((1, 8), (2, 4)), jnp.float32),
        "down_master": noise(keys[5], (EXPERTS, H, D), H ** -0.5, 0.1875, ((1, 8), (2, 4)), jnp.float32),
        "gate_first": noise(keys[6], (EXPERTS, H, D), 10.0, 60.0, ((1, 8), (2, 4)), jnp.float32),
        "up_first": noise(keys[7], (EXPERTS, H, D), 10.0, 60.0, ((1, 8), (2, 4)), jnp.float32),
        "down_first": noise(keys[8], (EXPERTS, H, D), 10.0, 60.0, ((1, 8), (2, 4)), jnp.float32),
        "gate_second": jnp.clip(jnp.exp(math.log(1000.0) - 2.3025851 * jax.random.uniform(keys[9], (EXPERTS, H, D), jnp.float32) ** block_scale(keys[9], (EXPERTS, H, D), ((1, 8), (2, 4)), -0.2, 0.2)), 100.0, 1000.0),
        "up_second": jnp.clip(jnp.exp(math.log(1000.0) - 2.3025851 * jax.random.uniform(keys[10], (EXPERTS, H, D), jnp.float32) ** block_scale(keys[10], (EXPERTS, H, D), ((1, 8), (2, 4)), -0.2, 0.2)), 100.0, 1000.0),
        "down_second": jnp.clip(jnp.exp(math.log(1000.0) - 2.3025851 * jax.random.uniform(keys[11], (EXPERTS, H, D), jnp.float32) ** block_scale(keys[11], (EXPERTS, H, D), ((1, 8), (2, 4)), -0.2, 0.2)), 100.0, 1000.0),
    }


beta_first = 0.9
beta_second = 0.95
learn_rate = 0.01
decay_rate = 0.1
epsilon = 1e-08

def adam_update(master, first, second, grads):
    first_new = beta_first * first + (1.0 - beta_first) * grads
    second_new = beta_second * second + (1.0 - beta_second) * grads * grads
    master_new = master - learn_rate * (first_new / (jnp.sqrt(second_new) + epsilon) + decay_rate * master)
    return (master_new, first_new, second_new)

def rounded(value):
    return lax.optimization_barrier(value.astype(jnp.bfloat16)).astype(jnp.float32)

def expert_pass(inputs, incoming, live, gate_w, up_w, down_w):
    position = jnp.arange(CAP, dtype=jnp.int32)
    keep = (position < live).astype(jnp.float32)
    gate_pre = jnp.dot(inputs, gate_w.T, preferred_element_type=jnp.float32)
    up_pre = jnp.dot(inputs, up_w.T, preferred_element_type=jnp.float32)
    hidden = (jax.nn.silu(gate_pre) * up_pre).astype(jnp.bfloat16)
    width = H // N_CUTS
    summed = jnp.zeros((CAP, D), jnp.float32)
    for block in range(N_CUTS):
        low = block * width
        part = jnp.dot(hidden[:, low:low + width], down_w[low:low + width], preferred_element_type=jnp.float32)
        summed = summed + rounded(part)
    outputs = (summed * keep[:, None]).astype(jnp.bfloat16)
    upstream = incoming * keep[:, None].astype(jnp.bfloat16)
    grad_hidden = jnp.dot(upstream, down_w.T, preferred_element_type=jnp.float32)
    sigmoid_gate = jax.nn.sigmoid(gate_pre)
    d_gate = (grad_hidden * up_pre * sigmoid_gate * (1.0 + gate_pre * (1.0 - sigmoid_gate))).astype(jnp.bfloat16)
    d_up = (grad_hidden * (gate_pre * sigmoid_gate)).astype(jnp.bfloat16)
    back = jnp.zeros((CAP, D), jnp.float32)
    for block in range(N_CUTS):
        low = block * width
        part = jnp.dot(d_gate[:, low:low + width], gate_w[low:low + width], preferred_element_type=jnp.float32)
        part = part + jnp.dot(d_up[:, low:low + width], up_w[low:low + width], preferred_element_type=jnp.float32)
        back = back + rounded(part)
    grad_gate = jnp.dot(d_gate.T, inputs, preferred_element_type=jnp.float32)
    grad_up = jnp.dot(d_up.T, inputs, preferred_element_type=jnp.float32)
    grad_down = jnp.dot(hidden.T, upstream, preferred_element_type=jnp.float32)
    return (outputs, back.astype(jnp.bfloat16), grad_gate, grad_up, grad_down)

def reference(token_rows, cotangent, counts, gate_master, up_master, down_master, gate_first, up_first, down_first, gate_second, up_second, down_second):
    outs_list = []
    backs_list = []
    gates_list = []
    ups_list = []
    downs_list = []
    for expert in range(EXPERTS):
        results = expert_pass(token_rows[expert], cotangent[expert], counts[expert], gate_master[expert].astype(jnp.bfloat16), up_master[expert].astype(jnp.bfloat16), down_master[expert].astype(jnp.bfloat16))
        outs_list.append(results[0])
        backs_list.append(results[1])
        gates_list.append(results[2])
        ups_list.append(results[3])
        downs_list.append(results[4])
    out_rows = jnp.stack(outs_list)
    input_grads = jnp.stack(backs_list)
    gate_new = adam_update(gate_master, gate_first, gate_second, jnp.stack(gates_list))
    up_new = adam_update(up_master, up_first, up_second, jnp.stack(ups_list))
    down_new = adam_update(down_master, down_first, down_second, jnp.stack(downs_list))
    return (out_rows, input_grads, gate_new[0], up_new[0], down_new[0], gate_new[1], up_new[1], down_new[1], gate_new[2], up_new[2], down_new[2])
```

```python
import jax
import jax.numpy as jnp
from jax import lax
from jax.sharding import PartitionSpec as P

beta_first = 0.9
beta_second = 0.95
learn_rate = 0.01
decay_rate = 0.1
epsilon = 1e-08


def adam_update(master, first, second, grads):
    master, grads = lax.optimization_barrier((master, grads))
    grads = grads.astype(jnp.float32)
    first_new = beta_first * first + (1.0 - beta_first) * grads
    second_new = beta_second * second + (1.0 - beta_second) * grads * grads
    master_new = master - learn_rate * (
        first_new / (jnp.sqrt(second_new) + epsilon) + decay_rate * master
    )
    return (master_new, first_new, second_new)


def dot_t(a, b):
    return lax.dot_general(a, b, (((1,), (1,)), ((), ())), preferred_element_type=jnp.float32)


def dot_n(a, b):
    return lax.dot_general(a, b, (((1,), (0,)), ((), ())), preferred_element_type=jnp.float32)


def dot_0(a, b):
    return lax.dot_general(a, b, (((0,), (0,)), ((), ())), preferred_element_type=jnp.float32)


def device_at(core, place, chips):
    chip = place if core == 0 else chips - 1 - place
    return 2 * chip + core


def hop(value, way, chips):
    pairs = []
    for core in range(2):
        for place in range(chips):
            last = place == chips - 1
            here = device_at(core, place, chips)
            there = device_at(1 - core if last else core, 0 if last else place + 1, chips)
            pairs.append((here, there) if way == 1 else (there, here))
    return lax.ppermute(value, "cuts", pairs)


def swap_cores(value, chips):
    pairs = [(2 * s + c, 2 * s + 1 - c) for s in range(chips) for c in range(2)]
    return lax.ppermute(value, "cuts", pairs)


def partner(index, turn, count):
    if count & (count - 1) == 0:
        return index ^ turn
    return (turn - index) % count


def plan_line(n):
    have = [{("T", p): None, ("C", p): None} for p in range(n)]
    made = [{} for _ in range(n)]
    came = {1: [{} for _ in range(n)], -1: [{} for _ in range(n)]}
    sends, works = [], []
    need = {}
    for d in (1, -1):
        for p in range(n):
            if 0 <= p + d < n:
                before = [b for b in range(n) if (b - p) * d <= 0]
                after = [b for b in range(n) if (b - p) * d > 0]
                need[d, p] = [("T", b) for b in sorted(before, key=lambda b: abs(b - p))]
                need[d, p] += [("C", b) for b in sorted(before, key=lambda b: -abs(b - p))]
                need[d, p] += [("O", b) for b in sorted(after, key=lambda b: -abs(b - p))]
                need[d, p] += [("I", b) for b in sorted(after, key=lambda b: -abs(b - p))]
    todo = [{k: [b for b in range(n) if b != p] for k in "TC"} for p in range(n)]

    def rank(p, kind, b):
        long_side = (b > p) == (2 * p < n - 1)
        return (not long_side, abs(b - p) if kind == "T" else -abs(b - p))

    step = 0
    while any(need.values()) or any(t[k] for t in todo for k in "TC"):
        sent, work = {}, {}
        for (d, p), left in need.items():
            for m in left:
                kind, b = m
                if kind in "TC":
                    ready = m in have[p]
                    terms = (have[p].get(m, ("own", kind)) or ("own", kind), None)
                else:
                    first = not 0 <= p - d < n
                    ready = b in made[p].get(kind, {}) and (first or m in came[d][p])
                    if ready:
                        terms = (made[p][kind][b], None if first else came[d][p][m])
                if ready:
                    sent[d, p] = (m, terms)
                    left.remove(m)
                    break
        for p in range(n):
            for kind in "TC":
                if kind == "C" and step < n:
                    continue
                can = [b for b in todo[p][kind] if (kind, b) in have[p]]
                if can:
                    b = min(can, key=lambda b: rank(p, kind, b))
                    todo[p][kind].remove(b)
                    work[kind, p] = (b, have[p][kind, b])
        for (d, p), (m, _) in sent.items():
            name = ("got", d, step)
            if m[0] in "TC":
                have[p + d][m] = name
            else:
                came[d][p + d][m] = name
        for (kind, p), (b, _) in work.items():
            made[p].setdefault({"T": "O", "C": "I"}[kind], {})[b] = ("made", kind, step)
        sends.append(sent)
        works.append(work)
        step += 1
    return sends, works, came


def pick(place, options, like):
    values = []
    for p, value in options.items():
        for entry in values:
            if entry[0] is value:
                entry[1].append(p)
                break
        else:
            values.append((value, [p]))
    if not values:
        return like
    values.sort(key=lambda entry: len(entry[1]))
    result = values[-1][0]
    for value, places in values[:-1]:
        here = place == places[0]
        for p in places[1:]:
            here = here | (place == p)
        result = jnp.where(here, value, result)
    return result


def make_shards(chips, experts):
    sends, works, came = plan_line(chips)

    def shards(
        token_rows, cotangent, counts,
        gate_master, up_master, down_master,
        gate_first, up_first, down_first,
        gate_second, up_second, down_second,
    ):
        local_rows = token_rows.shape[1]
        cut = lax.axis_index("cuts")
        core = cut % 2
        place = jnp.where(core == 0, cut // 2, chips - 1 - cut // 2)
        live = counts[lax.axis_index("expert")]
        own_row = jnp.arange(local_rows, dtype=jnp.int32) + cut * local_rows
        keep = (own_row < live)[:, None]
        own_t = token_rows[0]
        own_c = jnp.where(keep, cotangent[0], jnp.zeros_like(cotangent[0]))

        me = lax.axis_index("expert")
        cols = gate_master.shape[2]

        def fetch(master):
            whole = jnp.zeros((master.shape[1], experts * cols), jnp.bfloat16)
            for turn in range(experts):
                other = partner(me, turn, experts)
                piece = lax.dynamic_index_in_dim(master, other, 0, keepdims=False).astype(jnp.bfloat16)
                if turn:
                    pairs = [(e, partner(e, turn, experts)) for e in range(experts)]
                    piece = lax.ppermute(piece, "expert", pairs)
                whole = lax.dynamic_update_slice(whole, piece, (0, other * cols))
            return jnp.concatenate([whole, swap_cores(whole, chips)], axis=0)

        gate_w, up_w, down_w = fetch(gate_master), fetch(up_master), fetch(down_master)

        def forward(block):
            gate_pre = dot_t(block, gate_w)
            up_pre = dot_t(block, up_w)
            hidden = (gate_pre * jax.nn.sigmoid(gate_pre) * up_pre).astype(jnp.bfloat16)
            return gate_pre, up_pre, hidden, dot_n(hidden, down_w).astype(jnp.bfloat16)

        def backward(block, gate_pre, up_pre):
            grad_hidden = dot_t(block, down_w)
            sig = jax.nn.sigmoid(gate_pre)
            d_gate = (grad_hidden * up_pre * sig * (1.0 + gate_pre * (1.0 - sig))).astype(jnp.bfloat16)
            d_up = (grad_hidden * (gate_pre * sig)).astype(jnp.bfloat16)
            return d_gate, d_up, (dot_n(d_gate, gate_w) + dot_n(d_up, up_w)).astype(jnp.bfloat16)

        arrays = {("own", "T"): own_t, ("own", "C"): own_c}
        own_gate, own_up, own_hidden, own_out = forward(own_t)
        own_dg, own_du, own_back = backward(own_c, own_gate, own_up)
        t_work = [("own", {p: p for p in range(chips)})]
        c_work = [("own", {p: p for p in range(chips)})]
        t_got, c_got = {"own": (own_t, own_gate, own_up, own_hidden)}, {"own": (own_c, own_dg, own_du)}

        def of_block(wanted, steps, got, item):
            where_made = {}
            for p, b in wanted.items():
                for name, blocks in steps:
                    if blocks.get(p) == b:
                        where_made[p] = got[name][item]
            result = pick(place, where_made, None)
            idle = [p for p in range(chips) if p not in wanted]
            for p in idle:
                result = jnp.where(place == p, jnp.zeros_like(result), result)
            return result

        last_sent = None
        for step, (sent, work) in enumerate(zip(sends, works)):
            for d in (1, -1):
                before = ("got", d, step - 1)
                if before in arrays:
                    arrays[before] = lax.optimization_barrier((arrays[before], last_sent))[0]
                firsts = {p: arrays[terms[0]] for (e, p), (_, terms) in sent.items() if e == d}
                if not firsts:
                    continue
                value = pick(place, firsts, None)
                seconds = {p: arrays[terms[1]] for (e, p), (_, terms) in sent.items() if e == d and terms[1]}
                if seconds:
                    more = pick(place, seconds, None).astype(jnp.float32)
                    here = jnp.zeros((), jnp.bool_)
                    for p in seconds:
                        here = here | (place == p)
                    more = jnp.where(here, more, jnp.zeros_like(more))
                    value = (value.astype(jnp.float32) + more).astype(jnp.bfloat16)
                last_sent = value
                came_in = hop(value, d, chips)
                arrays["got", d, step] = came_in
            for kind in "TC":
                blocks = {p: b for (k, p), (b, _) in work.items() if k == kind}
                if not blocks:
                    continue
                block = pick(place, {p: arrays[name] for (k, p), (_, name) in work.items() if k == kind}, None)
                if kind == "T":
                    gate_pre, up_pre, hidden, out = forward(block)
                    t_work.append((step, blocks))
                    t_got[step] = (block, gate_pre, up_pre, hidden)
                    arrays["made", "T", step] = out
                else:
                    gate_pre, up_pre = of_block(blocks, t_work, t_got, 1), of_block(blocks, t_work, t_got, 2)
                    d_gate, d_up, back = backward(block, gate_pre, up_pre)
                    c_work.append((step, blocks))
                    c_got[step] = (block, d_gate, d_up)
                    arrays["made", "C", step] = back

        def total(own, kind):
            result = own.astype(jnp.float32)
            for d in (1, -1):
                ends = {}
                for p in range(chips):
                    name = came[d][p].get((kind, p))
                    if name:
                        ends.setdefault(name, []).append(p)
                for name, places in ends.items():
                    here = place == places[0]
                    for p in places[1:]:
                        here = here | (place == p)
                    value = arrays[name].astype(jnp.float32)
                    result = result + jnp.where(here, value, jnp.zeros_like(value))
            return result

        out_rows = jnp.where(keep, total(own_out, "O"), 0.0).astype(jnp.bfloat16)[None]
        input_grads = total(own_back, "I").astype(jnp.bfloat16)[None]

        tokens = jnp.concatenate([t_got[name][0] for name, _ in t_work], axis=0)
        upstream = jnp.concatenate([c_got[name][0] for name, _ in c_work], axis=0)
        hidden = jnp.concatenate([of_block(blocks, t_work, t_got, 3) for _, blocks in c_work], axis=0)
        d_gate = jnp.concatenate([of_block(blocks, c_work, c_got, 1) for _, blocks in t_work], axis=0)
        d_up = jnp.concatenate([of_block(blocks, c_work, c_got, 2) for _, blocks in t_work], axis=0)

        def collect(left, right):
            grad = dot_0(left, right).astype(jnp.bfloat16)
            units = grad.shape[0] // 2
            total = grad[:units].astype(jnp.float32) + swap_cores(grad[units:], chips).astype(jnp.float32)
            cols = total.shape[1] // experts
            pieces = total.astype(jnp.bfloat16).reshape(units, experts, cols).transpose(1, 0, 2)
            return lax.all_to_all(pieces, "expert", split_axis=0, concat_axis=0, tiled=True)

        grad_down = collect(hidden, upstream)
        grad_gate = collect(d_gate, tokens)
        grad_up = collect(d_up, tokens)
        down_new = adam_update(down_master, down_first, down_second, grad_down)
        gate_new = adam_update(gate_master, gate_first, gate_second, grad_gate)
        up_new = adam_update(up_master, up_first, up_second, grad_up)
        return (
            out_rows, input_grads,
            gate_new[0], up_new[0], down_new[0],
            gate_new[1], up_new[1], down_new[1],
            gate_new[2], up_new[2], down_new[2],
        )

    return shards


def solution(mesh):
    rows, states = P("expert", "cuts", None), P(None, "cuts", "expert")
    chips = mesh.shape["cuts"] // 2
    shards = make_shards(chips, mesh.shape["expert"])

    return jax.shard_map(
        shards,
        mesh=mesh,
        in_specs=(rows, rows, P()) + (states,) * 9,
        out_specs=(rows, rows) + (states,) * 9,
        check_vma=False,
    )
```

```python
import functools
import jax
import jax.numpy as jnp
from jax import lax
from jax.experimental import pallas as pl
from jax.experimental.pallas import tpu as pltpu
from jax.sharding import PartitionSpec as P

beta_first = 0.9
beta_second = 0.95
learn_rate = 0.01
decay_rate = 0.1
epsilon = 1e-08


def adam_kernel(count, order_ref, *refs):
    pieces, (master, first, second) = refs[:count], refs[count:count + 3]
    new_master, new_first, new_second = refs[count + 3:]
    turn = pl.program_id(0)
    grads = pieces[0][...].astype(jnp.float32)
    for other in range(1, count):
        grads = jnp.where(turn == other, pieces[other][...].astype(jnp.float32), grads)
    first_new = beta_first * first[0] + (1.0 - beta_first) * grads
    second_new = beta_second * second[0] + (1.0 - beta_second) * grads * grads
    new_master[0] = master[0] - learn_rate * (
        first_new / (jnp.sqrt(second_new) + epsilon) + decay_rate * master[0]
    )
    new_first[0] = first_new
    new_second[0] = second_new


def adam_update(order, pieces, master, first, second):
    count, units, cols = master.shape
    state = pl.BlockSpec((1, units, cols), lambda t, order: (order[t], 0, 0))
    piece = pl.BlockSpec((units, cols), lambda t, order: (0, 0))
    return pl.pallas_call(
        functools.partial(adam_kernel, count),
        grid_spec=pltpu.PrefetchScalarGridSpec(
            num_scalar_prefetch=1,
            grid=(count,),
            in_specs=[piece] * count + [state] * 3,
            out_specs=[state] * 3,
        ),
        out_shape=[jax.ShapeDtypeStruct(master.shape, jnp.float32)] * 3,
        compiler_params=pltpu.CompilerParams(vmem_limit_bytes=20 << 20),
        cost_estimate=pl.CostEstimate(
            flops=16 * master.size, transcendentals=master.size, bytes_accessed=26 * master.size
        ),
        name="adam",
    )(order, *pieces, master, first, second)


def join_kernel(count, order_ref, *refs):
    turn = pl.program_id(0)
    value = refs[0][...]
    for other in range(1, count):
        value = jnp.where(turn == other, refs[other][...], value)
    refs[count][...] = value


def join(order, pieces):
    count, (units, cols) = len(pieces), pieces[0].shape
    return pl.pallas_call(
        functools.partial(join_kernel, count),
        grid_spec=pltpu.PrefetchScalarGridSpec(
            num_scalar_prefetch=1,
            grid=(count,),
            in_specs=[pl.BlockSpec((units, cols), lambda t, order: (0, 0))] * count,
            out_specs=pl.BlockSpec((units, cols), lambda t, order: (0, order[t])),
        ),
        out_shape=jax.ShapeDtypeStruct((units, count * cols), pieces[0].dtype),
        compiler_params=pltpu.CompilerParams(vmem_limit_bytes=8 << 20),
        cost_estimate=pl.CostEstimate(
            flops=0, transcendentals=0, bytes_accessed=4 * count * units * cols
        ),
        name="join",
    )(order, *pieces)


def dot_t(a, b):
    return lax.dot_general(a, b, (((1,), (1,)), ((), ())), preferred_element_type=jnp.float32)


def dot_n(a, b):
    return lax.dot_general(a, b, (((1,), (0,)), ((), ())), preferred_element_type=jnp.float32)


def dot_0(a, b):
    return lax.dot_general(a, b, (((0,), (0,)), ((), ())), preferred_element_type=jnp.float32)


def device_at(core, place, chips):
    chip = place if core == 0 else chips - 1 - place
    return 2 * chip + core


def hop(value, way, chips):
    pairs = []
    for core in range(2):
        for place in range(chips):
            last = place == chips - 1
            here = device_at(core, place, chips)
            there = device_at(1 - core if last else core, 0 if last else place + 1, chips)
            pairs.append((here, there) if way == 1 else (there, here))
    return lax.ppermute(value, "cuts", pairs)


def swap_cores(value, chips):
    pairs = [(2 * s + c, 2 * s + 1 - c) for s in range(chips) for c in range(2)]
    return lax.ppermute(value, "cuts", pairs)


def partner(index, turn, count):
    if count & (count - 1) == 0:
        return index ^ turn
    return (turn - index) % count


def plan_line(n):
    have = [{("T", p): None, ("C", p): None} for p in range(n)]
    made = [{} for _ in range(n)]
    came = {1: [{} for _ in range(n)], -1: [{} for _ in range(n)]}
    sends, works = [], []
    need = {}
    for d in (1, -1):
        for p in range(n):
            if 0 <= p + d < n:
                before = [b for b in range(n) if (b - p) * d <= 0]
                after = [b for b in range(n) if (b - p) * d > 0]
                need[d, p] = [("T", b) for b in sorted(before, key=lambda b: abs(b - p))]
                need[d, p] += [("C", b) for b in sorted(before, key=lambda b: -abs(b - p))]
                need[d, p] += [("O", b) for b in sorted(after, key=lambda b: -abs(b - p))]
                need[d, p] += [("I", b) for b in sorted(after, key=lambda b: -abs(b - p))]
    todo = [{k: [b for b in range(n) if b != p] for k in "TC"} for p in range(n)]

    def rank(p, kind, b):
        long_side = (b > p) == (2 * p < n - 1)
        return (not long_side, abs(b - p) if kind == "T" else -abs(b - p))

    step = 0
    while any(need.values()) or any(t[k] for t in todo for k in "TC"):
        sent, work = {}, {}
        for (d, p), left in need.items():
            for m in left:
                kind, b = m
                if kind in "TC":
                    ready = m in have[p]
                    terms = (have[p].get(m, ("own", kind)) or ("own", kind), None)
                else:
                    first = not 0 <= p - d < n
                    ready = b in made[p].get(kind, {}) and (first or m in came[d][p])
                    if ready:
                        terms = (made[p][kind][b], None if first else came[d][p][m])
                if ready:
                    sent[d, p] = (m, terms)
                    left.remove(m)
                    break
        for p in range(n):
            for kind in "TC":
                if kind == "C" and step < n:
                    continue
                can = [b for b in todo[p][kind] if (kind, b) in have[p]]
                if can:
                    b = min(can, key=lambda b: rank(p, kind, b))
                    todo[p][kind].remove(b)
                    work[kind, p] = (b, have[p][kind, b])
        for (d, p), (m, _) in sent.items():
            name = ("got", d, step)
            if m[0] in "TC":
                have[p + d][m] = name
            else:
                came[d][p + d][m] = name
        for (kind, p), (b, _) in work.items():
            made[p].setdefault({"T": "O", "C": "I"}[kind], {})[b] = ("made", kind, step)
        sends.append(sent)
        works.append(work)
        step += 1
    return sends, works, came


def pick(place, options, like):
    values = []
    for p, value in options.items():
        for entry in values:
            if entry[0] is value:
                entry[1].append(p)
                break
        else:
            values.append((value, [p]))
    if not values:
        return like
    values.sort(key=lambda entry: len(entry[1]))
    result = values[-1][0]
    for value, places in values[:-1]:
        here = place == places[0]
        for p in places[1:]:
            here = here | (place == p)
        result = jnp.where(here, value, result)
    return result


def make_shards(chips, experts):
    sends, works, came = plan_line(chips)

    def shards(
        token_rows, cotangent, counts,
        gate_master, up_master, down_master,
        gate_first, up_first, down_first,
        gate_second, up_second, down_second,
    ):
        local_rows = token_rows.shape[1]
        cut = lax.axis_index("cuts")
        core = cut % 2
        place = jnp.where(core == 0, cut // 2, chips - 1 - cut // 2)
        live = counts[lax.axis_index("expert")]
        own_row = jnp.arange(local_rows, dtype=jnp.int32) + cut * local_rows
        keep = (own_row < live)[:, None]
        own_t = token_rows[0]
        own_c = jnp.where(keep, cotangent[0], jnp.zeros_like(cotangent[0]))
        own_c = lax.optimization_barrier(own_c)

        me = lax.axis_index("expert")
        cols = gate_master.shape[2]

        order = jnp.stack([partner(me, turn, experts) for turn in range(experts)]).astype(jnp.int32)

        def trade(pieces):
            return [pieces[0]] + [
                lax.ppermute(pieces[turn], "expert", [(e, partner(e, turn, experts)) for e in range(experts)])
                for turn in range(1, experts)
            ]

        def fetch(master):
            pieces = [
                lax.dynamic_index_in_dim(master, order[turn], 0, keepdims=False).astype(jnp.bfloat16)
                for turn in range(experts)
            ]
            pieces = trade(pieces)
            whole = join(order, pieces)
            both = jnp.concatenate([whole, swap_cores(whole, chips)], axis=0)
            return lax.optimization_barrier(both)

        gate_w, up_w, down_w = fetch(gate_master), fetch(up_master), fetch(down_master)

        def forward(block):
            gate_pre = dot_t(block, gate_w)
            up_pre = dot_t(block, up_w)
            hidden = (gate_pre * jax.nn.sigmoid(gate_pre) * up_pre).astype(jnp.bfloat16)
            return gate_pre, up_pre, hidden, dot_n(hidden, down_w).astype(jnp.bfloat16)

        def backward(block, gate_pre, up_pre):
            grad_hidden = dot_t(block, down_w)
            sig = jax.nn.sigmoid(gate_pre)
            d_gate = (grad_hidden * up_pre * sig * (1.0 + gate_pre * (1.0 - sig))).astype(jnp.bfloat16)
            d_up = (grad_hidden * (gate_pre * sig)).astype(jnp.bfloat16)
            return d_gate, d_up, (dot_n(d_gate, gate_w) + dot_n(d_up, up_w)).astype(jnp.bfloat16)

        arrays = {("own", "T"): own_t, ("own", "C"): own_c}
        t_work, c_work, t_got, c_got = [], [], {}, {}
        own_places = {p: p for p in range(chips)}
        t_steps = [i for i, work in enumerate(works) if any(k == "T" for k, _ in work)]
        c_steps = [i for i, work in enumerate(works) if any(k == "C" for k, _ in work)]
        own_with = {"T": t_steps[len(t_steps) // 2], "C": c_steps[len(c_steps) // 2]}

        def of_block(wanted, steps, got, item):
            where_made = {}
            for p, b in wanted.items():
                for name, blocks in steps:
                    if blocks.get(p) == b:
                        where_made[p] = got[name][item]
            result = pick(place, where_made, None)
            idle = [p for p in range(chips) if p not in wanted]
            for p in idle:
                result = jnp.where(place == p, jnp.zeros_like(result), result)
            return result

        last_sent = own_t
        for step, (sent, work) in enumerate(zip(sends, works)):
            for d in (1, -1):
                before = ("got", d, step - 1)
                if before in arrays:
                    arrays[before] = lax.optimization_barrier((arrays[before], last_sent))[0]
                firsts = {p: arrays[terms[0]] for (e, p), (_, terms) in sent.items() if e == d}
                if not firsts:
                    continue
                value = pick(place, firsts, None)
                seconds = {p: arrays[terms[1]] for (e, p), (_, terms) in sent.items() if e == d and terms[1]}
                if seconds:
                    more = pick(place, seconds, None)
                    here = jnp.zeros((), jnp.bool_)
                    for p in seconds:
                        here = here | (place == p)
                    more = jnp.where(here, more, jnp.zeros_like(more))
                    value = value + more
                last_sent = value
                came_in = hop(value, d, chips)
                arrays["got", d, step] = came_in
            for kind in "TC":
                blocks = {p: b for (k, p), (b, _) in work.items() if k == kind}
                if not blocks:
                    continue
                block = pick(place, {p: arrays[name] for (k, p), (_, name) in work.items() if k == kind}, None)
                with_own = own_with[kind] == step
                batch = [(step, blocks, block)]
                if with_own:
                    batch.append(("own", own_places, arrays["own", kind]))
                joined = jnp.concatenate([entry[2] for entry in batch], axis=0)
                if kind == "T":
                    results = forward(joined)
                else:
                    pres = [
                        jnp.concatenate([of_block(entry[1], t_work, t_got, item) for entry in batch], axis=0)
                        for item in (1, 2)
                    ]
                    results = backward(joined, *pres)
                results = [jnp.split(value, len(batch), axis=0) for value in results]
                for i, (name, its_blocks, its_block) in enumerate(batch):
                    mine = [value[i] for value in results]
                    mine[-1] = lax.optimization_barrier(mine[-1])
                    (t_work if kind == "T" else c_work).append((name, its_blocks))
                    (t_got if kind == "T" else c_got)[name] = (its_block, *mine)
                    arrays["made", kind, name] = mine[-1]

        def total(own, kind):
            result = lax.optimization_barrier((own, last_sent))[0].astype(jnp.float32)
            ends = {p: [came[d][p][kind, p] for d in (1, -1) if (kind, p) in came[d][p]] for p in range(chips)}
            for turn in range(2):
                terms = {p: arrays[names[turn]] for p, names in ends.items() if len(names) > turn}
                if not terms:
                    continue
                uses = {}
                for p, value in terms.items():
                    uses.setdefault(id(value), (value, []))[1].append(p)
                late = {}
                for value, places in uses.values():
                    value = lax.optimization_barrier((value, last_sent))[0]
                    late.update({p: value for p in places})
                more = pick(place, late, None)
                if len(late) < chips:
                    here = jnp.zeros((), jnp.bool_)
                    for p in late:
                        here = here | (place == p)
                    more = jnp.where(here, more, jnp.zeros_like(more))
                result = result + more.astype(jnp.float32)
            return result

        out_rows = jnp.where(keep, total(arrays["made", "T", "own"], "O"), 0.0).astype(jnp.bfloat16)[None]
        input_grads = total(arrays["made", "C", "own"], "I").astype(jnp.bfloat16)[None]

        tokens = jnp.concatenate([t_got[name][0] for name, _ in t_work], axis=0)
        upstream = jnp.concatenate([c_got[name][0] for name, _ in c_work], axis=0)
        hidden = jnp.concatenate([of_block(blocks, t_work, t_got, 3) for _, blocks in c_work], axis=0)
        d_gate = jnp.concatenate([of_block(blocks, c_work, c_got, 1) for _, blocks in t_work], axis=0)
        d_up = jnp.concatenate([of_block(blocks, c_work, c_got, 2) for _, blocks in t_work], axis=0)

        def collect(left, right):
            grad = dot_0(left, right).astype(jnp.bfloat16)
            units = grad.shape[0] // 2
            summed = grad[:units].astype(jnp.float32) + swap_cores(grad[units:], chips).astype(jnp.float32)
            summed = summed.astype(jnp.bfloat16)
            pieces = [
                lax.dynamic_slice_in_dim(summed, order[turn] * cols, cols, axis=1) for turn in range(experts)
            ]
            return trade(pieces)

        down_grads = collect(hidden, upstream)
        gate_grads = collect(d_gate, tokens)
        up_grads = collect(d_up, tokens)
        down_new = adam_update(order, down_grads, down_master, down_first, down_second)
        gate_new = adam_update(order, gate_grads, gate_master, gate_first, gate_second)
        up_new = adam_update(order, up_grads, up_master, up_first, up_second)
        return (
            out_rows, input_grads,
            gate_new[0], up_new[0], down_new[0],
            gate_new[1], up_new[1], down_new[1],
            gate_new[2], up_new[2], down_new[2],
        )

    return shards


def solution(mesh):
    rows, states = P("expert", "cuts", None), P(None, "cuts", "expert")
    chips = mesh.shape["cuts"] // 2
    shards = make_shards(chips, mesh.shape["expert"])

    return jax.shard_map(
        shards,
        mesh=mesh,
        in_specs=(rows, rows, P()) + (states,) * 9,
        out_specs=(rows, rows) + (states,) * 9,
        check_vma=False,
    )
```

```python
import functools
import jax
import jax.numpy as jnp
from jax import lax
from jax.experimental import pallas as pl
from jax.experimental.pallas import tpu as pltpu
from jax.sharding import PartitionSpec as P

beta_first = 0.9
beta_second = 0.95
learn_rate = 0.01
decay_rate = 0.1
epsilon = 1e-08


def adam_kernel(count, order_ref, *refs):
    pieces, (master, first, second) = refs[:count], refs[count:count + 3]
    new_master, new_first, new_second = refs[count + 3:]
    turn = pl.program_id(0)
    grads = pieces[0][...].astype(jnp.float32)
    for other in range(1, count):
        grads = jnp.where(turn == other, pieces[other][...].astype(jnp.float32), grads)
    first_new = beta_first * first[0] + (1.0 - beta_first) * grads
    second_new = beta_second * second[0] + (1.0 - beta_second) * grads * grads
    new_master[0] = master[0] - learn_rate * (
        first_new / (jnp.sqrt(second_new) + epsilon) + decay_rate * master[0]
    )
    new_first[0] = first_new
    new_second[0] = second_new


def adam_update(order, pieces, master, first, second):
    count, units, cols = master.shape
    state = pl.BlockSpec((1, units, cols), lambda t, order: (order[t], 0, 0))
    piece = pl.BlockSpec((units, cols), lambda t, order: (0, 0))
    return pl.pallas_call(
        functools.partial(adam_kernel, count),
        grid_spec=pltpu.PrefetchScalarGridSpec(
            num_scalar_prefetch=1,
            grid=(count,),
            in_specs=[piece] * count + [state] * 3,
            out_specs=[state] * 3,
        ),
        out_shape=[jax.ShapeDtypeStruct(master.shape, jnp.float32)] * 3,
        compiler_params=pltpu.CompilerParams(vmem_limit_bytes=20 << 20),
        cost_estimate=pl.CostEstimate(
            flops=16 * master.size, transcendentals=master.size, bytes_accessed=26 * master.size
        ),
        name="adam",
    )(order, *pieces, master, first, second)


def join_kernel(count, order_ref, *refs):
    turn = pl.program_id(0)
    value = refs[0][...]
    for other in range(1, count):
        value = jnp.where(turn == other, refs[other][...], value)
    refs[count][...] = value


def join(order, pieces):
    count, (units, cols) = len(pieces), pieces[0].shape
    return pl.pallas_call(
        functools.partial(join_kernel, count),
        grid_spec=pltpu.PrefetchScalarGridSpec(
            num_scalar_prefetch=1,
            grid=(count,),
            in_specs=[pl.BlockSpec((units, cols), lambda t, order: (0, 0))] * count,
            out_specs=pl.BlockSpec((units, cols), lambda t, order: (0, order[t])),
        ),
        out_shape=jax.ShapeDtypeStruct((units, count * cols), pieces[0].dtype),
        compiler_params=pltpu.CompilerParams(vmem_limit_bytes=8 << 20),
        cost_estimate=pl.CostEstimate(
            flops=0, transcendentals=0, bytes_accessed=4 * count * units * cols
        ),
        name="join",
    )(order, *pieces)


def dot_t(a, b):
    return lax.dot_general(a, b, (((1,), (1,)), ((), ())), preferred_element_type=jnp.float32)


def dot_n(a, b):
    return lax.dot_general(a, b, (((1,), (0,)), ((), ())), preferred_element_type=jnp.float32)


def dot_0(a, b):
    return lax.dot_general(a, b, (((0,), (0,)), ((), ())), preferred_element_type=jnp.float32)


STREAMS = 2


def device_at(core, place, chips):
    chip = place if core == 0 else chips - 1 - place
    return 2 * chip + core


def hop(value, way, chips):
    pairs = []
    for core in range(2):
        for place in range(chips):
            last = place == chips - 1
            here = device_at(core, place, chips)
            there = device_at(1 - core if last else core, 0 if last else place + 1, chips)
            pairs.append((here, there) if way == 1 else (there, here))
    return lax.ppermute(value, "cuts", pairs)


def swap_cores(value, chips):
    pairs = [(2 * s + c, 2 * s + 1 - c) for s in range(chips) for c in range(2)]
    return lax.ppermute(value, "cuts", pairs)


def partner(index, turn, count):
    if count & (count - 1) == 0:
        return index ^ turn
    return (turn - index) % count


def plan_line(n):
    have = [{("T", p): None, ("C", p): None} for p in range(n)]
    made = [{} for _ in range(n)]
    came = {1: [{} for _ in range(n)], -1: [{} for _ in range(n)]}
    sends, works = [], []
    need = {}
    for d in (1, -1):
        for p in range(n):
            if 0 <= p + d < n:
                before = [b for b in range(n) if (b - p) * d <= 0]
                after = [b for b in range(n) if (b - p) * d > 0]
                need[d, p] = [("T", b) for b in sorted(before, key=lambda b: abs(b - p))]
                need[d, p] += [("C", b) for b in sorted(before, key=lambda b: -abs(b - p))]
                need[d, p] += [("O", b) for b in sorted(after, key=lambda b: -abs(b - p))]
                need[d, p] += [("I", b) for b in sorted(after, key=lambda b: -abs(b - p))]
    todo = [{k: [b for b in range(n) if b != p] for k in "TC"} for p in range(n)]

    def rank(p, kind, b):
        long_side = (b > p) == (2 * p < n - 1)
        return (not long_side, abs(b - p) if kind == "T" else -abs(b - p))

    step = 0
    while any(need.values()) or any(t[k] for t in todo for k in "TC"):
        sent, work = {}, {}
        for (d, p), left in need.items():
            for m in left:
                kind, b = m
                if kind in "TC":
                    ready = m in have[p]
                    terms = (have[p].get(m, ("own", kind)) or ("own", kind), None)
                else:
                    first = not 0 <= p - d < n
                    ready = b in made[p].get(kind, {}) and (first or m in came[d][p])
                    if ready:
                        terms = (made[p][kind][b], None if first else came[d][p][m])
                if ready:
                    sent[d, p] = (m, terms)
                    left.remove(m)
                    break
        for p in range(n):
            for kind in "TC":
                if kind == "C" and step < n:
                    continue
                can = [b for b in todo[p][kind] if (kind, b) in have[p]]
                if can:
                    b = min(can, key=lambda b: rank(p, kind, b))
                    todo[p][kind].remove(b)
                    work[kind, p] = (b, have[p][kind, b])
        for (d, p), (m, _) in sent.items():
            name = ("got", d, step)
            if m[0] in "TC":
                have[p + d][m] = name
            else:
                came[d][p + d][m] = name
        for (kind, p), (b, _) in work.items():
            made[p].setdefault({"T": "O", "C": "I"}[kind], {})[b] = ("made", kind, step)
        sends.append(sent)
        works.append(work)
        step += 1
    return sends, works, came


def pick(place, options, like):
    values = []
    for p, value in options.items():
        for entry in values:
            if entry[0] is value:
                entry[1].append(p)
                break
        else:
            values.append((value, [p]))
    if not values:
        return like
    values.sort(key=lambda entry: len(entry[1]))
    result = values[-1][0]
    for value, places in values[:-1]:
        here = place == places[0]
        for p in places[1:]:
            here = here | (place == p)
        result = jnp.where(here, value, result)
    return result


def make_shards(chips, experts):
    sends, works, came = plan_line(chips)

    def shards(
        token_rows, cotangent, counts,
        gate_master, up_master, down_master,
        gate_first, up_first, down_first,
        gate_second, up_second, down_second,
    ):
        local_rows = token_rows.shape[1]
        cut = lax.axis_index("cuts")
        core = cut % 2
        place = jnp.where(core == 0, cut // 2, chips - 1 - cut // 2)
        live = counts[lax.axis_index("expert")]
        own_row = jnp.arange(local_rows, dtype=jnp.int32) + cut * local_rows
        keep = (own_row < live)[:, None]
        own_t = token_rows[0]
        own_c = cotangent[0]

        def live_rows(blocks):
            block = jnp.int32(0)
            for p, b in blocks.items():
                block = jnp.where(place == p, b, block)
            owner = jnp.where(core == 0, 2 * block, 2 * (chips - 1 - block) + 1)
            return (jnp.arange(local_rows, dtype=jnp.int32) + owner * local_rows < live)[:, None]

        me = lax.axis_index("expert")
        cols = gate_master.shape[2]

        order = jnp.stack([partner(me, turn, experts) for turn in range(experts)]).astype(jnp.int32)

        def trade(pieces):
            return [pieces[0]] + [
                lax.ppermute(pieces[turn], "expert", [(e, partner(e, turn, experts)) for e in range(experts)])
                for turn in range(1, experts)
            ]

        def fetch(master):
            pieces = [
                lax.dynamic_index_in_dim(master, order[turn], 0, keepdims=False).astype(jnp.bfloat16)
                for turn in range(experts)
            ]
            pieces = trade(pieces)
            whole = join(order, pieces)
            both = jnp.concatenate([whole, swap_cores(whole, chips)], axis=0)
            return lax.optimization_barrier(both)

        gate_w, up_w, down_w = fetch(gate_master), fetch(up_master), fetch(down_master)

        def forward(block):
            gate_pre = dot_t(block, gate_w)
            up_pre = dot_t(block, up_w)
            hidden = (gate_pre * jax.nn.sigmoid(gate_pre) * up_pre).astype(jnp.bfloat16)
            return gate_pre, up_pre, hidden, dot_n(hidden, down_w).astype(jnp.bfloat16)

        def backward(block, alive, gate_pre, up_pre):
            grad_hidden = jnp.where(alive, dot_t(block, down_w), 0.0)
            sig = jax.nn.sigmoid(gate_pre)
            d_gate = (grad_hidden * up_pre * sig * (1.0 + gate_pre * (1.0 - sig))).astype(jnp.bfloat16)
            d_up = (grad_hidden * (gate_pre * sig)).astype(jnp.bfloat16)
            return d_gate, d_up, (dot_n(d_gate, gate_w) + dot_n(d_up, up_w)).astype(jnp.bfloat16)

        whole = {("own", "T"): own_t, ("own", "C"): own_c}
        arrays = {}

        def part(name, q):
            if (name, q) not in arrays:
                width = whole[name].shape[1] // STREAMS
                arrays[name, q] = lax.slice_in_dim(whole[name], q * width, (q + 1) * width, axis=1)
            return arrays[name, q]

        t_work, c_work, t_got, c_got = [], [], {}, {}
        own_places = {p: p for p in range(chips)}
        t_steps = [i for i, work in enumerate(works) if any(k == "T" for k, _ in work)]
        c_steps = [i for i, work in enumerate(works) if any(k == "C" for k, _ in work)]
        own_with = {"T": t_steps[len(t_steps) // 2], "C": c_steps[len(c_steps) // 2]}

        def of_block(wanted, steps, got, item):
            where_made = {}
            for p, b in wanted.items():
                for name, blocks in steps:
                    if blocks.get(p) == b:
                        where_made[p] = got[name][item]
            result = pick(place, where_made, None)
            idle = [p for p in range(chips) if p not in wanted]
            for p in idle:
                result = jnp.where(place == p, jnp.zeros_like(result), result)
            return result

        last_sent = own_t
        for step, (sent, work) in enumerate(zip(sends, works)):
            for q in range(STREAMS):
                for d in (1, -1):
                    before = (("got", d, step - 1), q)
                    if before in arrays:
                        arrays[before] = lax.optimization_barrier((arrays[before], last_sent))[0]
                    firsts = {p: part(terms[0], q) for (e, p), (_, terms) in sent.items() if e == d}
                    if not firsts:
                        continue
                    value = pick(place, firsts, None)
                    seconds = {p: part(terms[1], q) for (e, p), (_, terms) in sent.items() if e == d and terms[1]}
                    if seconds:
                        more = pick(place, seconds, None)
                        here = jnp.zeros((), jnp.bool_)
                        for p in seconds:
                            here = here | (place == p)
                        more = jnp.where(here, more, jnp.zeros_like(more))
                        value = value + more
                    last_sent = value
                    arrays[("got", d, step), q] = hop(value, d, chips)
            for kind in "TC":
                blocks = {p: b for (k, p), (b, _) in work.items() if k == kind}
                if not blocks:
                    continue
                names = {p: name for (k, p), (_, name) in work.items() if k == kind}
                block = jnp.concatenate(
                    [pick(place, {p: part(name, q) for p, name in names.items()}, None) for q in range(STREAMS)],
                    axis=1,
                )
                if STREAMS > 1:
                    block = lax.optimization_barrier(block)
                with_own = own_with[kind] == step
                batch = [(step, blocks, block)]
                if with_own:
                    batch.append(("own", own_places, whole["own", kind]))
                joined = jnp.concatenate([entry[2] for entry in batch], axis=0)
                if kind == "T":
                    results = forward(joined)
                else:
                    pres = [
                        jnp.concatenate([of_block(entry[1], t_work, t_got, item) for entry in batch], axis=0)
                        for item in (1, 2)
                    ]
                    alive = jnp.concatenate([live_rows(entry[1]) for entry in batch], axis=0)
                    results = backward(joined, alive, *pres)
                results = [jnp.split(value, len(batch), axis=0) for value in results]
                for i, (name, its_blocks, its_block) in enumerate(batch):
                    mine = [value[i] for value in results]
                    mine[-1] = lax.optimization_barrier(mine[-1])
                    (t_work if kind == "T" else c_work).append((name, its_blocks))
                    (t_got if kind == "T" else c_got)[name] = (its_block, *mine)
                    whole["made", kind, name] = mine[-1]

        def total(kind, q):
            result = lax.optimization_barrier((part(("made", {"O": "T", "I": "C"}[kind], "own"), q), last_sent))[0]
            result = result.astype(jnp.float32)
            ends = {p: [came[d][p][kind, p] for d in (1, -1) if (kind, p) in came[d][p]] for p in range(chips)}
            for turn in range(2):
                late = {}
                for name in dict.fromkeys(names[turn] for names in ends.values() if len(names) > turn):
                    value = lax.optimization_barrier((part(name, q), last_sent))[0]
                    late.update({p: value for p, names in ends.items() if names[turn:turn + 1] == [name]})
                if not late:
                    continue
                more = pick(place, late, None)
                if len(late) < chips:
                    here = jnp.zeros((), jnp.bool_)
                    for p in late:
                        here = here | (place == p)
                    more = jnp.where(here, more, jnp.zeros_like(more))
                result = result + more.astype(jnp.float32)
            return result

        outs = [jnp.where(keep, total("O", q), 0.0).astype(jnp.bfloat16) for q in range(STREAMS)]
        out_rows = jnp.concatenate(outs, axis=1)[None]
        backs = [total("I", q).astype(jnp.bfloat16) for q in range(STREAMS)]
        input_grads = jnp.concatenate(backs, axis=1)[None]

        tokens = jnp.concatenate([t_got[name][0] for name, _ in t_work], axis=0)
        upstream = jnp.concatenate([c_got[name][0] for name, _ in c_work], axis=0)
        hidden = [jnp.where(live_rows(blocks), of_block(blocks, t_work, t_got, 3), 0) for _, blocks in c_work]
        hidden = jnp.concatenate(hidden, axis=0)
        d_gate = jnp.concatenate([of_block(blocks, c_work, c_got, 1) for _, blocks in t_work], axis=0)
        d_up = jnp.concatenate([of_block(blocks, c_work, c_got, 2) for _, blocks in t_work], axis=0)

        def collect(left, right):
            grad = dot_0(left, right).astype(jnp.bfloat16)
            units = grad.shape[0] // 2
            summed = grad[:units].astype(jnp.float32) + swap_cores(grad[units:], chips).astype(jnp.float32)
            summed = summed.astype(jnp.bfloat16)
            pieces = [
                lax.dynamic_slice_in_dim(summed, order[turn] * cols, cols, axis=1) for turn in range(experts)
            ]
            return trade(pieces)

        down_grads = collect(hidden, upstream)
        gate_grads = collect(d_gate, tokens)
        up_grads = collect(d_up, tokens)
        down_new = adam_update(order, down_grads, down_master, down_first, down_second)
        gate_new = adam_update(order, gate_grads, gate_master, gate_first, gate_second)
        up_new = adam_update(order, up_grads, up_master, up_first, up_second)
        return (
            out_rows, input_grads,
            gate_new[0], up_new[0], down_new[0],
            gate_new[1], up_new[1], down_new[1],
            gate_new[2], up_new[2], down_new[2],
        )

    return shards


def solution(mesh):
    rows, states = P("expert", "cuts", None), P(None, "cuts", "expert")
    chips = mesh.shape["cuts"] // 2
    shards = make_shards(chips, mesh.shape["expert"])

    return jax.shard_map(
        shards,
        mesh=mesh,
        in_specs=(rows, rows, P()) + (states,) * 9,
        out_specs=(rows, rows) + (states,) * 9,
        check_vma=False,
    )
```

```python
import functools
import jax
import jax.numpy as jnp
from jax import lax
from jax.experimental import pallas as pl
from jax.experimental.pallas import tpu as pltpu
from jax.sharding import PartitionSpec as P

beta_first = 0.9
beta_second = 0.95
learn_rate = 0.01
decay_rate = 0.1
epsilon = 1e-08


def adam_kernel(count, order_ref, *refs):
    pieces, (master, first, second) = refs[:count], refs[count:count + 3]
    new_master, new_first, new_second = refs[-3:]
    turn = pl.program_id(0)
    grads = pieces[0][...].astype(jnp.float32)
    for other in range(1, count):
        grads = jnp.where(turn == other, pieces[other][...].astype(jnp.float32), grads)
    first_new = beta_first * first[0] + (1.0 - beta_first) * grads
    second_new = beta_second * second[0] + (1.0 - beta_second) * grads * grads
    new_master[0] = master[0] - learn_rate * (
        first_new / (jnp.sqrt(second_new) + epsilon) + decay_rate * master[0]
    )
    new_first[0] = first_new
    new_second[0] = second_new


def adam_update(order, pieces, master, first, second, calls=1):
    count, units, cols = master.shape
    calls = calls if count % calls == 0 else 1
    turns = count // calls
    done = []
    for call in range(calls):
        low = call * turns
        state = pl.BlockSpec((1, units, cols), lambda t, order, low=low: (order[t + low], 0, 0))
        piece = pl.BlockSpec((units, cols), lambda t, order: (0, 0))
        done = pl.pallas_call(
            functools.partial(adam_kernel, turns),
            grid_spec=pltpu.PrefetchScalarGridSpec(
                num_scalar_prefetch=1,
                grid=(turns,),
                in_specs=[piece] * turns + [state] * 3 + [pl.BlockSpec(memory_space=pl.ANY)] * len(done),
                out_specs=[state] * 3,
            ),
            out_shape=[jax.ShapeDtypeStruct(master.shape, jnp.float32)] * 3,
            input_output_aliases={turns + 4 + i: i for i in range(len(done))},
            compiler_params=pltpu.CompilerParams(vmem_limit_bytes=20 << 20),
            cost_estimate=pl.CostEstimate(
                flops=16 * master.size // calls,
                transcendentals=master.size // calls,
                bytes_accessed=26 * master.size // calls,
            ),
            name="adam",
        )(order, *pieces[low:low + turns], master, first, second, *done)
    return done


def join_kernel(count, order_ref, *refs):
    turn = pl.program_id(0)
    value = refs[0][...]
    for other in range(1, count):
        value = jnp.where(turn == other, refs[other][...], value)
    refs[count][...] = value


def join(order, pieces):
    count, (units, cols) = len(pieces), pieces[0].shape
    return pl.pallas_call(
        functools.partial(join_kernel, count),
        grid_spec=pltpu.PrefetchScalarGridSpec(
            num_scalar_prefetch=1,
            grid=(count,),
            in_specs=[pl.BlockSpec((units, cols), lambda t, order: (0, 0))] * count,
            out_specs=pl.BlockSpec((units, cols), lambda t, order: (0, order[t])),
        ),
        out_shape=jax.ShapeDtypeStruct((units, count * cols), pieces[0].dtype),
        compiler_params=pltpu.CompilerParams(vmem_limit_bytes=8 << 20),
        cost_estimate=pl.CostEstimate(
            flops=0, transcendentals=0, bytes_accessed=4 * count * units * cols
        ),
        name="join",
    )(order, *pieces)


def dot_t(a, b):
    return lax.dot_general(a, b, (((1,), (1,)), ((), ())), preferred_element_type=jnp.float32)


def dot_n(a, b):
    return lax.dot_general(a, b, (((1,), (0,)), ((), ())), preferred_element_type=jnp.float32)


def dot_0(a, b):
    return lax.dot_general(a, b, (((0,), (0,)), ((), ())), preferred_element_type=jnp.float32)


STREAMS = 2


def device_at(core, place, chips):
    chip = place if core == 0 else chips - 1 - place
    return 2 * chip + core


def hop(value, way, chips):
    pairs = []
    for core in range(2):
        for place in range(chips):
            last = place == chips - 1
            here = device_at(core, place, chips)
            there = device_at(1 - core if last else core, 0 if last else place + 1, chips)
            pairs.append((here, there) if way == 1 else (there, here))
    return lax.ppermute(value, "cuts", pairs)


def swap_cores(value, chips):
    pairs = [(2 * s + c, 2 * s + 1 - c) for s in range(chips) for c in range(2)]
    return lax.ppermute(value, "cuts", pairs)


def partner(index, turn, count):
    if count & (count - 1) == 0:
        return index ^ turn
    return (turn - index) % count


def plan_line(n):
    have = [{("T", p): None, ("C", p): None} for p in range(n)]
    made = [{} for _ in range(n)]
    came = {1: [{} for _ in range(n)], -1: [{} for _ in range(n)]}
    sends, works = [], []
    need = {}
    for d in (1, -1):
        for p in range(n):
            if 0 <= p + d < n:
                before = [b for b in range(n) if (b - p) * d <= 0]
                after = [b for b in range(n) if (b - p) * d > 0]
                need[d, p] = [("T", b) for b in sorted(before, key=lambda b: abs(b - p))]
                need[d, p] += [("C", b) for b in sorted(before, key=lambda b: -abs(b - p))]
                need[d, p] += [("O", b) for b in sorted(after, key=lambda b: -abs(b - p))]
                need[d, p] += [("I", b) for b in sorted(after, key=lambda b: -abs(b - p))]
    todo = [{k: [b for b in range(n) if b != p] for k in "TC"} for p in range(n)]

    def rank(p, kind, b):
        long_side = (b > p) == (2 * p < n - 1)
        return (not long_side, abs(b - p) if kind == "T" else -abs(b - p))

    step = 0
    while any(need.values()) or any(t[k] for t in todo for k in "TC"):
        sent, work = {}, {}
        for (d, p), left in need.items():
            for m in left:
                kind, b = m
                if kind in "TC":
                    ready = m in have[p]
                    terms = (have[p].get(m, ("own", kind)) or ("own", kind), None)
                else:
                    first = not 0 <= p - d < n
                    ready = b in made[p].get(kind, {}) and (first or m in came[d][p])
                    if ready:
                        terms = (made[p][kind][b], None if first else came[d][p][m])
                if ready:
                    sent[d, p] = (m, terms)
                    left.remove(m)
                    break
        for p in range(n):
            for kind in "TC":
                if kind == "C" and step < n:
                    continue
                can = [b for b in todo[p][kind] if (kind, b) in have[p]]
                if can:
                    b = min(can, key=lambda b: rank(p, kind, b))
                    todo[p][kind].remove(b)
                    work[kind, p] = (b, have[p][kind, b])
        for (d, p), (m, _) in sent.items():
            name = ("got", d, step)
            if m[0] in "TC":
                have[p + d][m] = name
            else:
                came[d][p + d][m] = name
        for (kind, p), (b, _) in work.items():
            made[p].setdefault({"T": "O", "C": "I"}[kind], {})[b] = ("made", kind, step)
        sends.append(sent)
        works.append(work)
        step += 1
    return sends, works, came


def pick(place, options, like):
    values = []
    for p, value in options.items():
        for entry in values:
            if entry[0] is value:
                entry[1].append(p)
                break
        else:
            values.append((value, [p]))
    if not values:
        return like
    values.sort(key=lambda entry: len(entry[1]))
    result = values[-1][0]
    for value, places in values[:-1]:
        here = place == places[0]
        for p in places[1:]:
            here = here | (place == p)
        result = jnp.where(here, value, result)
    return result


def make_shards(chips, experts):
    sends, works, came = plan_line(chips)

    def shards(
        token_rows, cotangent, counts,
        gate_master, up_master, down_master,
        gate_first, up_first, down_first,
        gate_second, up_second, down_second,
    ):
        local_rows = token_rows.shape[1]
        cut = lax.axis_index("cuts")
        core = cut % 2
        place = jnp.where(core == 0, cut // 2, chips - 1 - cut // 2)
        live = counts[lax.axis_index("expert")]
        own_row = jnp.arange(local_rows, dtype=jnp.int32) + cut * local_rows
        keep = (own_row < live)[:, None]
        own_t = token_rows[0]
        own_c = cotangent[0]

        def live_rows(blocks):
            block = jnp.int32(0)
            for p, b in blocks.items():
                block = jnp.where(place == p, b, block)
            owner = jnp.where(core == 0, 2 * block, 2 * (chips - 1 - block) + 1)
            return (jnp.arange(local_rows, dtype=jnp.int32) + owner * local_rows < live)[:, None]

        me = lax.axis_index("expert")
        cols = gate_master.shape[2]

        order = jnp.stack([partner(me, turn, experts) for turn in range(experts)]).astype(jnp.int32)

        def trade(pieces):
            return [pieces[0]] + [
                lax.ppermute(pieces[turn], "expert", [(e, partner(e, turn, experts)) for e in range(experts)])
                for turn in range(1, experts)
            ]

        def fetch(master):
            pieces = [
                lax.dynamic_index_in_dim(master, order[turn], 0, keepdims=False).astype(jnp.bfloat16)
                for turn in range(experts)
            ]
            pieces = trade(pieces)
            whole = join(order, pieces)
            partner_half = swap_cores(whole, chips)
            both = jnp.concatenate([whole, partner_half], axis=0)
            return lax.optimization_barrier(both)

        gate_w, up_w, down_w = fetch(gate_master), fetch(up_master), fetch(down_master)

        def forward(block):
            gate_pre = dot_t(block, gate_w)
            up_pre = dot_t(block, up_w)
            hidden = (gate_pre * jax.nn.sigmoid(gate_pre) * up_pre).astype(jnp.bfloat16)
            return gate_pre, up_pre, hidden, dot_n(hidden, down_w).astype(jnp.bfloat16)

        def backward(block, alive, gate_pre, up_pre):
            grad_hidden = jnp.where(alive, dot_t(block, down_w), 0.0)
            sig = jax.nn.sigmoid(gate_pre)
            d_gate = (grad_hidden * up_pre * sig * (1.0 + gate_pre * (1.0 - sig))).astype(jnp.bfloat16)
            d_up = (grad_hidden * (gate_pre * sig)).astype(jnp.bfloat16)
            return d_gate, d_up, (dot_n(d_gate, gate_w) + dot_n(d_up, up_w)).astype(jnp.bfloat16)

        whole = {("own", "T"): own_t, ("own", "C"): own_c}
        arrays = {}

        def part(name, q):
            if (name, q) not in arrays:
                width = whole[name].shape[1] // STREAMS
                arrays[name, q] = lax.slice_in_dim(whole[name], q * width, (q + 1) * width, axis=1)
            return arrays[name, q]

        t_work, c_work, t_got, c_got = [], [], {}, {}
        own_places = {p: p for p in range(chips)}
        t_steps = [i for i, work in enumerate(works) if any(k == "T" for k, _ in work)]
        c_steps = [i for i, work in enumerate(works) if any(k == "C" for k, _ in work)]
        own_with = {"T": t_steps[len(t_steps) // 2], "C": c_steps[len(c_steps) // 2]}

        def of_block(wanted, steps, got, item):
            where_made = {}
            for p, b in wanted.items():
                for name, blocks in steps:
                    if blocks.get(p) == b:
                        where_made[p] = got[name][item]
            result = pick(place, where_made, None)
            idle = [p for p in range(chips) if p not in wanted]
            for p in idle:
                result = jnp.where(place == p, jnp.zeros_like(result), result)
            return result

        last_sent = own_t
        for step, (sent, work) in enumerate(zip(sends, works)):
            for q in range(STREAMS):
                for d in (1, -1):
                    before = (("got", d, step - 1), q)
                    if before in arrays:
                        arrays[before] = lax.optimization_barrier((arrays[before], last_sent))[0]
                    firsts = {p: part(terms[0], q) for (e, p), (_, terms) in sent.items() if e == d}
                    if not firsts:
                        continue
                    value = pick(place, firsts, None)
                    seconds = {p: part(terms[1], q) for (e, p), (_, terms) in sent.items() if e == d and terms[1]}
                    if seconds:
                        more = pick(place, seconds, None)
                        here = jnp.zeros((), jnp.bool_)
                        for p in seconds:
                            here = here | (place == p)
                        more = jnp.where(here, more, jnp.zeros_like(more))
                        value = value + more
                    last_sent = value
                    arrays[("got", d, step), q] = hop(value, d, chips)
            for kind in "TC":
                blocks = {p: b for (k, p), (b, _) in work.items() if k == kind}
                if not blocks:
                    continue
                names = {p: name for (k, p), (_, name) in work.items() if k == kind}
                block = jnp.concatenate(
                    [pick(place, {p: part(name, q) for p, name in names.items()}, None) for q in range(STREAMS)],
                    axis=1,
                )
                if STREAMS > 1:
                    block = lax.optimization_barrier(block)
                with_own = own_with[kind] == step
                batch = [(step, blocks, block)]
                if with_own:
                    batch.append(("own", own_places, whole["own", kind]))
                joined = jnp.concatenate([entry[2] for entry in batch], axis=0)
                if kind == "T":
                    results = forward(joined)
                else:
                    pres = [
                        jnp.concatenate([of_block(entry[1], t_work, t_got, item) for entry in batch], axis=0)
                        for item in (1, 2)
                    ]
                    alive = jnp.concatenate([live_rows(entry[1]) for entry in batch], axis=0)
                    results = backward(joined, alive, *pres)
                results = [jnp.split(value, len(batch), axis=0) for value in results]
                for i, (name, its_blocks, its_block) in enumerate(batch):
                    mine = [value[i] for value in results]
                    mine[-1] = lax.optimization_barrier(mine[-1])
                    (t_work if kind == "T" else c_work).append((name, its_blocks))
                    (t_got if kind == "T" else c_got)[name] = (its_block, *mine)
                    whole["made", kind, name] = mine[-1]

        def total(kind, q):
            result = lax.optimization_barrier((part(("made", {"O": "T", "I": "C"}[kind], "own"), q), last_sent))[0]
            result = result.astype(jnp.float32)
            ends = {p: [came[d][p][kind, p] for d in (1, -1) if (kind, p) in came[d][p]] for p in range(chips)}
            for turn in range(2):
                late = {}
                for name in dict.fromkeys(names[turn] for names in ends.values() if len(names) > turn):
                    value = lax.optimization_barrier((part(name, q), last_sent))[0]
                    late.update({p: value for p, names in ends.items() if names[turn:turn + 1] == [name]})
                if not late:
                    continue
                more = pick(place, late, None)
                if len(late) < chips:
                    here = jnp.zeros((), jnp.bool_)
                    for p in late:
                        here = here | (place == p)
                    more = jnp.where(here, more, jnp.zeros_like(more))
                result = result + more.astype(jnp.float32)
            return result

        outs = [jnp.where(keep, total("O", q), 0.0).astype(jnp.bfloat16) for q in range(STREAMS)]
        out_rows = jnp.concatenate(outs, axis=1)[None]
        backs = [total("I", q).astype(jnp.bfloat16) for q in range(STREAMS)]
        input_grads = jnp.concatenate(backs, axis=1)[None]

        tokens = jnp.concatenate([t_got[name][0] for name, _ in t_work], axis=0)
        upstream = jnp.concatenate([c_got[name][0] for name, _ in c_work], axis=0)
        hidden = [jnp.where(live_rows(blocks), of_block(blocks, t_work, t_got, 3), 0) for _, blocks in c_work]
        hidden = jnp.concatenate(hidden, axis=0)
        d_gate = jnp.concatenate([of_block(blocks, c_work, c_got, 1) for _, blocks in t_work], axis=0)
        d_up = jnp.concatenate([of_block(blocks, c_work, c_got, 2) for _, blocks in t_work], axis=0)

        def collect(left, right):
            grad = dot_0(left, right).astype(jnp.bfloat16)
            units = grad.shape[0] // 2
            summed = grad[:units].astype(jnp.float32) + swap_cores(grad[units:], chips).astype(jnp.float32)
            summed = summed.astype(jnp.bfloat16)
            pieces = [
                lax.dynamic_slice_in_dim(summed, order[turn] * cols, cols, axis=1) for turn in range(experts)
            ]
            return trade(pieces)

        down_grads = collect(hidden, upstream)
        gate_grads = collect(d_gate, tokens)
        up_grads = collect(d_up, tokens)
        down_new = adam_update(order, down_grads, down_master, down_first, down_second)
        gate_new = adam_update(order, gate_grads, gate_master, gate_first, gate_second)
        up_new = adam_update(order, up_grads, up_master, up_first, up_second, calls=4)
        return (
            out_rows, input_grads,
            gate_new[0], up_new[0], down_new[0],
            gate_new[1], up_new[1], down_new[1],
            gate_new[2], up_new[2], down_new[2],
        )

    return shards


def solution(mesh):
    rows, states = P("expert", "cuts", None), P(None, "cuts", "expert")
    chips = mesh.shape["cuts"] // 2
    shards = make_shards(chips, mesh.shape["expert"])

    return jax.shard_map(
        shards,
        mesh=mesh,
        in_specs=(rows, rows, P()) + (states,) * 9,
        out_specs=(rows, rows) + (states,) * 9,
        check_vma=False,
    )
```
